32 devices in a mesh: grp: 4 (over x, core), vec: 8 (over z, y).
Axes of the slice: x: 2, y: 2, z: 4, core: 2. Of those that a mesh axis runs over, the one named last changes fastest.
Arguments:
- vv_vectors: bfloat16 [1280, 1000, 1000], P(('grp', 'vec')), may hold values from -0.1875 to 0.1875
- oo_vectors: bfloat16 [1280, 100, 100], P(('grp', 'vec')), may hold values from -0.625 to 0.625
- ov_slab: bfloat16 [1280, 1024], P(('grp', 'vec')), may hold values from -0.15625 to 0.15625
- amplitudes: bfloat16 [100, 1000], P('grp'), may hold values from -6 to 6
Outputs:
- sigma_slab: float32 [96000, 1024], P(('grp', 'vec'))
The draws below stay inside these ranges and needn't reach their ends.
All inputs are finite; a program needn't handle non-finite values.
Results may differ from the reference program's by a relative error of at most 0.0029.
Values may be sent and summed in bfloat16 or wider, within the bound.
A program may use at most 192 MiB of HBM per device.

```python
import math
import jax
import jax.numpy as jnp
from jax import lax

NO = 100
NV = 1000
NP = 1280
I_ROWS = 96
SLAB = 1024


def level_of(key, dims, split, low, largest):
    level = 1.0
    for axis_at, parts in split:
        heights = jax.random.uniform(jax.random.fold_in(jax.random.fold_in(key, 6), axis_at), (parts,), jnp.float32, low / len(split), largest / len(split))
        level = level * jnp.repeat(jnp.exp(heights), dims[axis_at] // parts).reshape((-1,) + (1,) * (len(dims) - 1 - axis_at))
    return level


def gaussian(own_key, extent, scale, reach, shards=(), held_as=jnp.bfloat16):
    entries = jax.random.normal(own_key, extent, jnp.float32) * scale
    if len(shards) > 0:
        entries = level_of(own_key, extent, shards, -0.22, 0.18) * entries
    return jnp.clip(entries, min=-reach, max=reach).astype(held_as)


def setup_inputs(seed: int = 0) -> dict:
    keys = jax.random.split(jax.random.key(seed), 5)
    vv_vectors = gaussian(keys[0], (NP, NV, NV), NV ** -0.5, 0.1875, ((0, 32),))
    oo_vectors = gaussian(keys[1], (NP, NO, NO), NO ** -0.5, 0.625, ((0, 32),))
    ov_slab = gaussian(keys[2], (NP, SLAB), NP ** -0.5, 0.15625, ((0, 32),))
    amplitudes = gaussian(keys[3], (NO, NV), 1.0, 6.0, ((0, 4),))
    return {"vv_vectors": vv_vectors, "oo_vectors": oo_vectors, "ov_slab": ov_slab, "amplitudes": amplitudes}


def reference(vv_vectors, oo_vectors, ov_slab, amplitudes):
    block_size = math.gcd(NP, 64)
    window = amplitudes[:I_ROWS].astype(jnp.float32)
    amps_all = amplitudes.astype(jnp.float32)

    def accumulate(running, counter):
        offset = (counter * block_size).astype(jnp.int32)
        vv_block = lax.dynamic_slice_in_dim(vv_vectors, offset, block_size, 0).astype(jnp.float32)
        oo_block = lax.dynamic_slice_in_dim(oo_vectors, offset, block_size, 0)[:, :, :I_ROWS].astype(jnp.float32)
        ov_part = lax.dynamic_slice_in_dim(ov_slab, offset, block_size, 0)
        direct_term = jnp.einsum('ib,pab->pia', window, vv_block)
        hole_term = jnp.einsum('pji,ja->pia', oo_block, amps_all)
        dressed = (direct_term - hole_term).astype(jnp.bfloat16).reshape(block_size, I_ROWS * NV)
        update = lax.dot_general(dressed, ov_part, (((0,), (0,)), ((), ())), preferred_element_type=jnp.float32)
        return running + update, None

    start_sum = jnp.zeros((I_ROWS * NV, SLAB), jnp.float32)
    running, _ = lax.scan(accumulate, start_sum, jnp.arange(NP // block_size, dtype=jnp.int32))
    return running
```

```python
import functools
import jax
import jax.numpy as jnp
from jax import lax
from jax.experimental import pallas as pl
from jax.experimental.pallas import tpu as pltpu
from jax.sharding import PartitionSpec as P

I_ROWS = 96
CHUNK = 8
SLOTS = 4
MESH = pl.DeviceIdType.MESH


def farthest_first(count):
    return sorted(range(count), key=lambda k: (abs(k - count // 2), k))


def exchange_kernel(
    ng, nv, inner, amps, oo, ov, vv, out, slab, vv_slots, stage, dressed,
    vv_sem, send_sem, recv_sem, own_sem, col_send, col_recv, plane_send, plane_recv, slab_sem,
):
    g = lax.axis_index("grp")
    v = lax.axis_index("vec")
    me = g * nv + v
    local_count, nvirt = vv.shape[0], vv.shape[1]
    chunks = local_count // CHUNK
    per = I_ROWS // (ng * nv)
    outer = nv // inner
    z = v // inner
    y = lax.rem(v, inner)
    offsets = [(dg, dv) for dv in farthest_first(nv) for dg in range(ng) if (dg, dv) != (0, 0)]
    plane = [(dg, dy) for dg in range(ng) for dy in range(inner) if (dg, dy) != (0, 0)]

    def load(p):
        slot = lax.rem(p, SLOTS)
        return pltpu.make_async_copy(vv.at[p], vv_slots.at[slot], vv_sem.at[slot])

    barrier = pltpu.get_barrier_semaphore()
    for dg, dv in offsets:
        pl.semaphore_signal(
            barrier, inc=1, device_id=(lax.rem(g + dg, ng), lax.rem(v + dv, nv)), device_id_type=MESH
        )
    for p in range(SLOTS):
        load(p).start()
    own_slab = pltpu.make_async_copy(ov, slab.at[g, z, y], slab_sem)
    own_slab.start()
    pl.semaphore_wait(barrier, len(offsets))

    def column_copy(dz):
        return pltpu.make_async_remote_copy(
            src_ref=ov,
            dst_ref=slab.at[g, z, y],
            send_sem=col_send.at[dz],
            recv_sem=col_recv.at[dz],
            device_id=(g, lax.rem(z + dz, outer) * inner + y),
            device_id_type=MESH,
        )

    def plane_copy(j):
        dg, dy = plane[j]
        return pltpu.make_async_remote_copy(
            src_ref=slab.at[g, :, y],
            dst_ref=slab.at[g, :, y],
            send_sem=plane_send.at[j],
            recv_sem=plane_recv.at[j],
            device_id=(lax.rem(g + dg, ng), z * inner + lax.rem(y + dy, inner)),
            device_id_type=MESH,
        )

    for dz in range(1, outer):
        column_copy(dz).start()

    @pl.loop(0, chunks)
    def _(c):
        @pl.loop(0, CHUNK)
        def _(k):
            p = c * CHUNK + k
            load(p).wait()
            direct = lax.dot_general(
                amps[0:I_ROWS, :], vv_slots[lax.rem(p, SLOTS)], (((1,), (1,)), ((), ())),
                preferred_element_type=jnp.float32,
            )
            hole = lax.dot_general(
                oo[p, :, 0:I_ROWS], amps[...], (((0,), (0,)), ((), ())), preferred_element_type=jnp.float32
            )
            value = direct - hole
            for t in range(stage.shape[0]):
                lo, hi = t * 128, min(t * 128 + 128, nvirt)
                stage[t, pl.ds(pl.multiple_of(k * I_ROWS, I_ROWS), I_ROWS), 0:hi - lo] = value[:, lo:hi]

            @pl.when(p + SLOTS < local_count)
            def _():
                load(p + SLOTS).start()

        for i in range(I_ROWS):
            for t in range(stage.shape[0]):
                lo, hi = t * 128, min(t * 128 + 128, nvirt)
                rows = stage[t, pl.ds(i, CHUNK, stride=I_ROWS), :]
                dressed[c, i, :, lo:hi] = rows[:, : hi - lo].astype(jnp.bfloat16)

        for j, (dg, dv) in enumerate(offsets):
            to_g = lax.rem(g + dg, ng)
            to_v = lax.rem(v + dv, nv)
            pltpu.make_async_remote_copy(
                src_ref=dressed.at[c, pl.ds((to_g * nv + to_v) * per, per)],
                dst_ref=out.at[:, me * chunks + c],
                send_sem=send_sem,
                recv_sem=recv_sem.at[j],
                device_id=(to_g, to_v),
                device_id_type=MESH,
            ).start()
        pltpu.make_async_copy(
            dressed.at[c, pl.ds(me * per, per)], out.at[:, me * chunks + c], own_sem
        ).start()

        @pl.when(c == 0)
        def _():
            own_slab.wait()
            for dz in range(1, outer):
                column_copy(dz).wait_send()
                column_copy(dz).wait_recv()
            for j in range(len(plane)):
                plane_copy(j).start()

    def block_wait(sem, source):
        ref = out.at[:, pl.ds(source * chunks, chunks)]
        pltpu.make_async_copy(ref, ref, sem).wait()

    for j in range(len(plane)):
        plane_copy(j).wait_send()
        plane_copy(j).wait_recv()
    everything = out.at[:, pl.ds(0, len(offsets) * chunks)]
    pltpu.make_async_copy(everything, everything, send_sem).wait()
    block_wait(own_sem, me)
    for j, (dg, dv) in enumerate(offsets):
        block_wait(recv_sem.at[j], lax.rem(g + ng - dg, ng) * nv + lax.rem(v + nv - dv, nv))


def exchange(ng, nv, vv_vectors, oo_vectors, ov_slab, amps_all):
    local_count, nvirt = vv_vectors.shape[0], vv_vectors.shape[1]
    devices = ng * nv
    inner = 2 if nv % 2 == 0 else 1
    outer = nv // inner
    chunks = local_count // CHUNK
    per = I_ROWS // devices
    lanes = -(-nvirt // 128) * 128
    anywhere = pl.BlockSpec(memory_space=pl.ANY)
    vmem = pl.BlockSpec(memory_space=pltpu.VMEM)
    dma = pltpu.SemaphoreType.DMA
    regrouped, slab = pl.pallas_call(
        functools.partial(exchange_kernel, ng, nv, inner),
        out_shape=(
            jax.ShapeDtypeStruct((per, devices * chunks, CHUNK, nvirt), jnp.bfloat16),
            jax.ShapeDtypeStruct((ng, outer, inner) + ov_slab.shape, jnp.bfloat16),
        ),
        in_specs=[vmem, vmem, anywhere, anywhere],
        out_specs=(anywhere, anywhere),
        scratch_shapes=[
            pltpu.VMEM((SLOTS, nvirt, nvirt), jnp.bfloat16),
            pltpu.VMEM((lanes // 128, CHUNK * I_ROWS, 128), jnp.float32),
            pltpu.VMEM((chunks, I_ROWS, CHUNK, nvirt), jnp.bfloat16),
            dma((SLOTS,)),
            dma,
            dma((devices - 1,)),
            dma,
            dma((outer,)),
            dma((outer,)),
            dma((ng * inner - 1,)),
            dma((ng * inner - 1,)),
            dma,
        ],
        compiler_params=pltpu.CompilerParams(
            collective_id=0, has_side_effects=True, vmem_limit_bytes=48 * 1024 * 1024
        ),
    )(amps_all, oo_vectors, ov_slab, vv_vectors)
    return regrouped.reshape(per, devices * local_count, nvirt), slab.reshape(-1, ov_slab.shape[1])


def plain(vv_vectors, oo_vectors, ov_slab, amps_all):
    local_count, nvirt = vv_vectors.shape[0], vv_vectors.shape[1]
    window = amps_all[:I_ROWS]
    direct_term = jnp.einsum("ib,pab->pia", window, vv_vectors, preferred_element_type=jnp.float32)
    hole_term = jnp.einsum(
        "pji,ja->pia", oo_vectors[:, :, :I_ROWS], amps_all, preferred_element_type=jnp.float32
    )
    dressed = (direct_term - hole_term).astype(jnp.bfloat16).reshape(local_count, I_ROWS * nvirt)
    regrouped = lax.all_to_all(dressed, ("grp", "vec"), split_axis=1, concat_axis=0, tiled=True)
    return lax.dot_general(
        regrouped,
        lax.all_gather(ov_slab, ("grp", "vec"), axis=0, tiled=True),
        (((0,), (0,)), ((), ())),
        preferred_element_type=jnp.float32,
    )


def solution(mesh):
    ng, nv = mesh.shape["grp"], mesh.shape["vec"]

    def shards(vv_vectors, oo_vectors, ov_slab, amplitudes):
        amps_all = lax.all_gather(amplitudes, "grp", axis=0, tiled=True)
        if I_ROWS % (ng * nv) or vv_vectors.shape[0] % CHUNK:
            return plain(vv_vectors, oo_vectors, ov_slab, amps_all)
        regrouped, slab = exchange(ng, nv, vv_vectors, oo_vectors, ov_slab, amps_all)
        sigma = lax.dot_general(
            regrouped, slab, (((1,), (0,)), ((), ())), preferred_element_type=jnp.float32
        )
        return sigma.reshape(-1, slab.shape[1])

    return jax.shard_map(
        shards,
        mesh=mesh,
        in_specs=(
            P(("grp", "vec"), None, None),
            P(("grp", "vec"), None, None),
            P(("grp", "vec"), None),
            P("grp", None),
        ),
        out_specs=P(("grp", "vec"), None),
        check_vma=False,
    )
```

```python
import functools
import jax
import jax.numpy as jnp
from jax import lax
from jax.experimental import pallas as pl
from jax.experimental.pallas import tpu as pltpu
from jax.sharding import PartitionSpec as P

I_ROWS = 96
CHUNK = 8
SLOTS = 4
COLUMNS = 256
LIMIT_MIB = 26
FINISH_MIB = 8
MESH = pl.DeviceIdType.MESH


def farthest_first(count):
    return sorted(range(count), key=lambda k: (abs(k - count // 2), k))


def exchange_kernel(
    ng, nv, inner, amps, oo, ov, vv, partial, received, slab,
    vv_slots, stage, dressed, gathered, rows_f32, amps_all,
    vv_sem, send_sem, recv_sem, own_sem, col_send, col_recv, plane_send, plane_recv, slab_sem,
    amps_send, amps_recv, amps_own,
):
    g = lax.axis_index("grp")
    v = lax.axis_index("vec")
    me = g * nv + v
    local_count, nvirt = vv.shape[0], vv.shape[1]
    chunks = local_count // CHUNK
    per = I_ROWS // (ng * nv)
    depth = ng * nv * CHUNK
    outer = nv // inner
    z = v // inner
    y = lax.rem(v, inner)
    held = amps.shape[0]
    offsets = [(dg, dv) for dv in farthest_first(nv) for dg in range(ng) if (dg, dv) != (0, 0)]
    plane = [(dg, dy) for dg in range(ng) for dy in range(inner) if (dg, dy) != (0, 0)]

    def load(p):
        slot = lax.rem(p, SLOTS)
        return pltpu.make_async_copy(vv.at[p], vv_slots.at[slot], vv_sem.at[slot])

    barrier = pltpu.get_barrier_semaphore()
    for dg, dv in offsets:
        pl.semaphore_signal(
            barrier, inc=1, device_id=(lax.rem(g + dg, ng), lax.rem(v + dv, nv)), device_id_type=MESH
        )
    for p in range(SLOTS):
        load(p).start()
    slab_here = slab.at[:, g, z, pl.ds(pl.multiple_of(y * CHUNK, CHUNK), CHUNK)]
    own_slab = pltpu.make_async_copy(ov, slab_here, slab_sem)
    own_slab.start()
    own_amps = pltpu.make_async_copy(amps, gathered.at[g], amps_own)
    own_amps.start()
    pl.semaphore_wait(barrier, len(offsets))

    def amps_copy(dg):
        return pltpu.make_async_remote_copy(
            src_ref=amps,
            dst_ref=gathered.at[g],
            send_sem=amps_send.at[dg],
            recv_sem=amps_recv.at[dg],
            device_id=(lax.rem(g + dg, ng), v),
            device_id_type=MESH,
        )

    def column_copy(dz):
        return pltpu.make_async_remote_copy(
            src_ref=ov,
            dst_ref=slab_here,
            send_sem=col_send.at[dz],
            recv_sem=col_recv.at[dz],
            device_id=(g, lax.rem(z + dz, outer) * inner + y),
            device_id_type=MESH,
        )

    def plane_copy(j):
        dg, dy = plane[j]
        column = slab.at[:, g, :, pl.ds(pl.multiple_of(y * CHUNK, CHUNK), CHUNK)]
        return pltpu.make_async_remote_copy(
            src_ref=column,
            dst_ref=column,
            send_sem=plane_send.at[j],
            recv_sem=plane_recv.at[j],
            device_id=(lax.rem(g + dg, ng), z * inner + lax.rem(y + dy, inner)),
            device_id_type=MESH,
        )

    for dg in range(1, ng):
        amps_copy(dg).start()
    for dz in range(1, outer):
        column_copy(dz).start()
    own_amps.wait()
    for dg in range(1, ng):
        amps_copy(dg).wait_send()
        amps_copy(dg).wait_recv()
    for s in range(ng):
        rows_f32[s * held:(s + 1) * held, :] = gathered[s].astype(jnp.float32)
    amps_all[...] = rows_f32[0:ng * held, :].astype(jnp.bfloat16)

    @pl.loop(0, chunks)
    def _(c):
        @pl.loop(0, CHUNK)
        def _(k):
            p = c * CHUNK + k
            load(p).wait()
            direct = lax.dot_general(
                amps_all[0:I_ROWS, :], vv_slots[lax.rem(p, SLOTS)], (((1,), (1,)), ((), ())),
                preferred_element_type=jnp.float32,
            )
            hole = lax.dot_general(
                oo[p, :, 0:I_ROWS], amps_all[...], (((0,), (0,)), ((), ())),
                preferred_element_type=jnp.float32,
            )
            value = direct - hole
            for t in range(stage.shape[0]):
                lo, hi = t * 128, min(t * 128 + 128, nvirt)
                stage[t, pl.ds(pl.multiple_of(k * I_ROWS, I_ROWS), I_ROWS), 0:hi - lo] = value[:, lo:hi]

            @pl.when(p + SLOTS < local_count)
            def _():
                load(p + SLOTS).start()

        for i in range(I_ROWS):
            for t in range(stage.shape[0]):
                lo, hi = t * 128, min(t * 128 + 128, nvirt)
                rows = stage[t, pl.ds(i, CHUNK, stride=I_ROWS), :]
                dressed[c, i, :, lo:hi] = rows[:, : hi - lo].astype(jnp.bfloat16)

        landing = received.at[c, :, pl.ds(pl.multiple_of(me * CHUNK, CHUNK), CHUNK)]
        for dg, dv in offsets:
            to_g = lax.rem(g + dg, ng)
            to_v = lax.rem(v + dv, nv)
            pltpu.make_async_remote_copy(
                src_ref=dressed.at[c, pl.ds((to_g * nv + to_v) * per, per)],
                dst_ref=landing,
                send_sem=send_sem,
                recv_sem=recv_sem.at[c],
                device_id=(to_g, to_v),
                device_id_type=MESH,
            ).start()
        pltpu.make_async_copy(dressed.at[c, pl.ds(me * per, per)], landing, own_sem.at[c]).start()

        @pl.when(c == 0)
        def _():
            own_slab.wait()
            for dz in range(1, outer):
                column_copy(dz).wait_send()
                column_copy(dz).wait_recv()
            for j in range(len(plane)):
                plane_copy(j).start()

    for j in range(len(plane)):
        plane_copy(j).wait_send()
        plane_copy(j).wait_recv()

    def arrived(c):
        others = received.at[c, :, pl.ds(0, depth - CHUNK)]
        pltpu.make_async_copy(others, others, recv_sem.at[c]).wait()
        mine = received.at[c, :, pl.ds(0, CHUNK)]
        pltpu.make_async_copy(mine, mine, own_sem.at[c]).wait()

    partial[...] = jnp.zeros_like(partial)

    @pl.loop(0, chunks - 1)
    def _(c):
        arrived(c)

        @pl.loop(0, per)
        def _(i):
            lhs = received[c, i]
            rhs = slab[c].reshape(depth, slab.shape[-1])
            for lo in range(0, slab.shape[-1], COLUMNS):
                partial[i, :, lo:lo + COLUMNS] += lax.dot_general(
                    lhs, rhs[:, lo:lo + COLUMNS], (((0,), (0,)), ((), ())),
                    preferred_element_type=jnp.float32,
                )

    arrived(chunks - 1)
    sent = received.at[:, :, pl.ds(0, depth - CHUNK)]
    pltpu.make_async_copy(sent, sent, send_sem).wait()


def finish_kernel(partial, received, slab, out):
    i, j = pl.program_id(0), pl.program_id(1)
    columns = pl.ds(pl.multiple_of(j * COLUMNS, COLUMNS), COLUMNS)
    last = received.shape[0] - 1
    rhs = slab[last, :, :, :, columns].reshape(received.shape[2], COLUMNS)
    out[0] = partial[i, :, columns] + lax.dot_general(
        received[last, i], rhs, (((0,), (0,)), ((), ())), preferred_element_type=jnp.float32
    )


def contract(ng, nv, vv_vectors, oo_vectors, ov_slab, amplitudes):
    local_count, nvirt = vv_vectors.shape[0], vv_vectors.shape[1]
    width = ov_slab.shape[1]
    devices = ng * nv
    inner = 2 if nv % 2 == 0 else 1
    outer = nv // inner
    chunks = local_count // CHUNK
    per = I_ROWS // devices
    lanes = -(-nvirt // 128) * 128
    nocc = ng * amplitudes.shape[0]
    anywhere = pl.BlockSpec(memory_space=pl.ANY)
    vmem = pl.BlockSpec(memory_space=pltpu.VMEM)
    dma = pltpu.SemaphoreType.DMA
    partial, received, slab = pl.pallas_call(
        functools.partial(exchange_kernel, ng, nv, inner),
        out_shape=(
            jax.ShapeDtypeStruct((per, nvirt, width), jnp.float32),
            jax.ShapeDtypeStruct((chunks, per, devices * CHUNK, nvirt), jnp.bfloat16),
            jax.ShapeDtypeStruct((chunks, ng, outer, inner * CHUNK, width), jnp.bfloat16),
        ),
        in_specs=[vmem, vmem, vmem, anywhere],
        out_specs=(vmem, vmem, vmem),
        scratch_shapes=[
            pltpu.VMEM((SLOTS, nvirt, nvirt), jnp.bfloat16),
            pltpu.VMEM((lanes // 128, CHUNK * I_ROWS, 128), jnp.float32),
            pltpu.VMEM((chunks, I_ROWS, CHUNK, nvirt), jnp.bfloat16),
            pltpu.VMEM((ng,) + amplitudes.shape, jnp.bfloat16),
            pltpu.VMEM((nocc, nvirt), jnp.float32),
            pltpu.VMEM((nocc, nvirt), jnp.bfloat16),
            dma((SLOTS,)),
            dma,
            dma((chunks,)),
            dma((chunks,)),
            dma((outer,)),
            dma((outer,)),
            dma((ng * inner - 1,)),
            dma((ng * inner - 1,)),
            dma,
            dma((ng,)),
            dma((ng,)),
            dma,
        ],
        compiler_params=pltpu.CompilerParams(
            collective_id=0, has_side_effects=True, vmem_limit_bytes=LIMIT_MIB * 1024 * 1024
        ),
    )(amplitudes, oo_vectors, ov_slab.reshape(chunks, CHUNK, width), vv_vectors)
    return pl.pallas_call(
        finish_kernel,
        out_shape=jax.ShapeDtypeStruct((per, nvirt, width), jnp.float32),
        grid=(per, width // COLUMNS),
        in_specs=[vmem, vmem, vmem],
        out_specs=pl.BlockSpec((1, nvirt, COLUMNS), lambda i, j: (i, 0, j)),
        compiler_params=pltpu.CompilerParams(vmem_limit_bytes=FINISH_MIB * 1024 * 1024),
    )(partial, received, slab).reshape(per * nvirt, width)


def plain(vv_vectors, oo_vectors, ov_slab, amps_all):
    local_count, nvirt = vv_vectors.shape[0], vv_vectors.shape[1]
    window = amps_all[:I_ROWS]
    direct_term = jnp.einsum("ib,pab->pia", window, vv_vectors, preferred_element_type=jnp.float32)
    hole_term = jnp.einsum(
        "pji,ja->pia", oo_vectors[:, :, :I_ROWS], amps_all, preferred_element_type=jnp.float32
    )
    dressed = (direct_term - hole_term).astype(jnp.bfloat16).reshape(local_count, I_ROWS * nvirt)
    regrouped = lax.all_to_all(dressed, ("grp", "vec"), split_axis=1, concat_axis=0, tiled=True)
    return lax.dot_general(
        regrouped,
        lax.all_gather(ov_slab, ("grp", "vec"), axis=0, tiled=True),
        (((0,), (0,)), ((), ())),
        preferred_element_type=jnp.float32,
    )


def solution(mesh):
    ng, nv = mesh.shape["grp"], mesh.shape["vec"]

    def shards(vv_vectors, oo_vectors, ov_slab, amplitudes):
        if I_ROWS % (ng * nv) or vv_vectors.shape[0] % CHUNK or ov_slab.shape[1] % COLUMNS:
            amps_all = lax.all_gather(amplitudes, "grp", axis=0, tiled=True)
            return plain(vv_vectors, oo_vectors, ov_slab, amps_all)
        return contract(ng, nv, vv_vectors, oo_vectors, ov_slab, amplitudes)

    return jax.shard_map(
        shards,
        mesh=mesh,
        in_specs=(
            P(("grp", "vec"), None, None),
            P(("grp", "vec"), None, None),
            P(("grp", "vec"), None),
            P("grp", None),
        ),
        out_specs=P(("grp", "vec"), None),
        check_vma=False,
    )
```

```python
import functools
import jax
import jax.numpy as jnp
from jax import lax
from jax.experimental import pallas as pl
from jax.experimental.pallas import tpu as pltpu
from jax.sharding import PartitionSpec as P

I_ROWS = 96
CHUNK = 8
SLOTS = 4
COLUMNS = 256
FINISH_COLUMNS = 512
LIMIT_MIB = 26
FINISH_MIB = 8
MESH = pl.DeviceIdType.MESH


def farthest_first(count):
    return sorted(range(count), key=lambda k: (abs(k - count // 2), k))


def exchange_kernel(
    ng, nv, inner, amps, oo, ov, vv, partial, received, slab,
    vv_slots, stage, dressed, gathered, rows_f32, amps_all,
    vv_sem, send_sem, recv_sem, own_sem, col_send, col_recv, plane_send, plane_recv, slab_sem,
    amps_send, amps_recv, amps_own,
):
    g = lax.axis_index("grp")
    v = lax.axis_index("vec")
    me = g * nv + v
    local_count, nvirt = vv.shape[0], vv.shape[1]
    chunks = local_count // CHUNK
    per = I_ROWS // (ng * nv)
    depth = ng * nv * CHUNK
    outer = nv // inner
    z = v // inner
    y = lax.rem(v, inner)
    held = amps.shape[0]
    offsets = [(dg, dv) for dv in farthest_first(nv) for dg in range(ng) if (dg, dv) != (0, 0)]
    plane = [(dg, dy) for dg in range(ng) for dy in range(inner) if (dg, dy) != (0, 0)]

    def load(p):
        slot = lax.rem(p, SLOTS)
        return pltpu.make_async_copy(vv.at[p], vv_slots.at[slot], vv_sem.at[slot])

    barrier = pltpu.get_barrier_semaphore()
    for dg, dv in offsets:
        pl.semaphore_signal(
            barrier, inc=1, device_id=(lax.rem(g + dg, ng), lax.rem(v + dv, nv)), device_id_type=MESH
        )
    for p in range(SLOTS):
        load(p).start()
    slab_here = slab.at[:, g, z, pl.ds(pl.multiple_of(y * CHUNK, CHUNK), CHUNK)]
    own_slab = pltpu.make_async_copy(ov, slab_here, slab_sem)
    own_slab.start()
    own_amps = pltpu.make_async_copy(amps, gathered.at[g], amps_own)
    own_amps.start()
    pl.semaphore_wait(barrier, len(offsets))

    def amps_copy(dg):
        return pltpu.make_async_remote_copy(
            src_ref=amps,
            dst_ref=gathered.at[g],
            send_sem=amps_send.at[dg],
            recv_sem=amps_recv.at[dg],
            device_id=(lax.rem(g + dg, ng), v),
            device_id_type=MESH,
        )

    def column_copy(dz):
        return pltpu.make_async_remote_copy(
            src_ref=ov,
            dst_ref=slab_here,
            send_sem=col_send.at[dz],
            recv_sem=col_recv.at[dz],
            device_id=(g, lax.rem(z + dz, outer) * inner + y),
            device_id_type=MESH,
        )

    def plane_copy(j):
        dg, dy = plane[j]
        column = slab.at[:, g, :, pl.ds(pl.multiple_of(y * CHUNK, CHUNK), CHUNK)]
        return pltpu.make_async_remote_copy(
            src_ref=column,
            dst_ref=column,
            send_sem=plane_send.at[j],
            recv_sem=plane_recv.at[j],
            device_id=(lax.rem(g + dg, ng), z * inner + lax.rem(y + dy, inner)),
            device_id_type=MESH,
        )

    for dg in range(1, ng):
        amps_copy(dg).start()
    for dz in range(1, outer):
        column_copy(dz).start()
    own_amps.wait()
    for dg in range(1, ng):
        amps_copy(dg).wait_send()
        amps_copy(dg).wait_recv()
    for s in range(ng):
        rows_f32[s * held:(s + 1) * held, :] = gathered[s].astype(jnp.float32)
    amps_all[...] = rows_f32[0:ng * held, :].astype(jnp.bfloat16)

    @pl.loop(0, chunks)
    def _(c):
        @pl.loop(0, CHUNK)
        def _(k):
            p = c * CHUNK + k
            load(p).wait()
            direct = lax.dot_general(
                amps_all[0:I_ROWS, :], vv_slots[lax.rem(p, SLOTS)], (((1,), (1,)), ((), ())),
                preferred_element_type=jnp.float32,
            )
            hole = lax.dot_general(
                oo[p, :, 0:I_ROWS], amps_all[...], (((0,), (0,)), ((), ())),
                preferred_element_type=jnp.float32,
            )
            value = direct - hole
            for t in range(stage.shape[0]):
                lo, hi = t * 128, min(t * 128 + 128, nvirt)
                stage[t, pl.ds(pl.multiple_of(k * I_ROWS, I_ROWS), I_ROWS), 0:hi - lo] = value[:, lo:hi]

            @pl.when(p + SLOTS < local_count)
            def _():
                load(p + SLOTS).start()

        landing = received.at[c, :, pl.ds(pl.multiple_of(me * CHUNK, CHUNK), CHUNK)]

        def owner(dv, dg):
            return lax.rem(g + dg, ng), lax.rem(v + nv + dv * (1 - 2 * lax.rem(g, 2)), nv)

        def regroup(first):
            for i in range(per):
                for t in range(stage.shape[0]):
                    lo, hi = t * 128, min(t * 128 + 128, nvirt)
                    rows = stage[t, pl.ds(first + i, CHUNK, stride=I_ROWS), :]
                    dressed[c, first + i, :, lo:hi] = rows[:, : hi - lo].astype(jnp.bfloat16)

        def send(dv, dg):
            to_g, to_v = owner(dv, dg)
            pltpu.make_async_remote_copy(
                src_ref=dressed.at[c, pl.ds((to_g * nv + to_v) * per, per)],
                dst_ref=landing,
                send_sem=send_sem,
                recv_sem=recv_sem.at[c],
                device_id=(to_g, to_v),
                device_id_type=MESH,
            ).start()

        order = [(dv, dg) for dv in range(1, nv) for dg in range(ng)] + [(0, dg) for dg in range(1, ng)]
        for at, step in enumerate(order):
            to_g, to_v = owner(*step)
            regroup((to_g * nv + to_v) * per)
            if at >= 2:
                send(*order[at - 2])
        regroup(me * per)
        send(*order[-2])
        send(*order[-1])
        pltpu.make_async_copy(dressed.at[c, pl.ds(me * per, per)], landing, own_sem.at[c]).start()

        @pl.when(c == 0)
        def _():
            own_slab.wait()
            for dz in range(1, outer):
                column_copy(dz).wait_send()
                column_copy(dz).wait_recv()
            for j in range(len(plane)):
                plane_copy(j).start()

    for j in range(len(plane)):
        plane_copy(j).wait_send()
        plane_copy(j).wait_recv()

    def arrived(c):
        others = received.at[c, :, pl.ds(0, depth - CHUNK)]
        pltpu.make_async_copy(others, others, recv_sem.at[c]).wait()
        mine = received.at[c, :, pl.ds(0, CHUNK)]
        pltpu.make_async_copy(mine, mine, own_sem.at[c]).wait()

    partial[...] = jnp.zeros_like(partial)

    @pl.loop(0, chunks - 1)
    def _(c):
        arrived(c)

        @pl.loop(0, per)
        def _(i):
            lhs = received[c, i]
            rhs = slab[c].reshape(depth, slab.shape[-1])
            for lo in range(0, slab.shape[-1], COLUMNS):
                partial[i, :, lo:lo + COLUMNS] += lax.dot_general(
                    lhs, rhs[:, lo:lo + COLUMNS], (((0,), (0,)), ((), ())),
                    preferred_element_type=jnp.float32,
                )

    arrived(chunks - 1)
    sent = received.at[:, :, pl.ds(0, depth - CHUNK)]
    pltpu.make_async_copy(sent, sent, send_sem).wait()


def finish_kernel(partial, received, slab, out):
    i, j = pl.program_id(0), pl.program_id(1)
    columns = pl.ds(pl.multiple_of(j * FINISH_COLUMNS, FINISH_COLUMNS), FINISH_COLUMNS)
    last = received.shape[0] - 1
    rhs = slab[last, :, :, :, columns].reshape(received.shape[2], FINISH_COLUMNS)
    out[0] = partial[i, :, columns] + lax.dot_general(
        received[last, i], rhs, (((0,), (0,)), ((), ())), preferred_element_type=jnp.float32
    )


def contract(ng, nv, vv_vectors, oo_vectors, ov_slab, amplitudes):
    local_count, nvirt = vv_vectors.shape[0], vv_vectors.shape[1]
    width = ov_slab.shape[1]
    devices = ng * nv
    inner = 2 if nv % 2 == 0 else 1
    outer = nv // inner
    chunks = local_count // CHUNK
    per = I_ROWS // devices
    lanes = -(-nvirt // 128) * 128
    nocc = ng * amplitudes.shape[0]
    hbm = pl.BlockSpec(memory_space=pltpu.HBM)
    vmem = pl.BlockSpec(memory_space=pltpu.VMEM)
    dma = pltpu.SemaphoreType.DMA
    partial, received, slab = pl.pallas_call(
        functools.partial(exchange_kernel, ng, nv, inner),
        out_shape=(
            jax.ShapeDtypeStruct((per, nvirt, width), jnp.float32),
            jax.ShapeDtypeStruct((chunks, per, devices * CHUNK, nvirt), jnp.bfloat16),
            jax.ShapeDtypeStruct((chunks, ng, outer, inner * CHUNK, width), jnp.bfloat16),
        ),
        in_specs=[hbm, vmem, hbm, hbm],
        out_specs=(vmem, vmem, vmem),
        scratch_shapes=[
            pltpu.VMEM((SLOTS, nvirt, nvirt), jnp.bfloat16),
            pltpu.VMEM((lanes // 128, CHUNK * I_ROWS, 128), jnp.float32),
            pltpu.VMEM((chunks, I_ROWS, CHUNK, nvirt), jnp.bfloat16),
            pltpu.VMEM((ng,) + amplitudes.shape, jnp.bfloat16),
            pltpu.VMEM((nocc, nvirt), jnp.float32),
            pltpu.VMEM((nocc, nvirt), jnp.bfloat16),
            dma((SLOTS,)),
            dma,
            dma((chunks,)),
            dma((chunks,)),
            dma((outer,)),
            dma((outer,)),
            dma((ng * inner - 1,)),
            dma((ng * inner - 1,)),
            dma,
            dma((ng,)),
            dma((ng,)),
            dma,
        ],
        compiler_params=pltpu.CompilerParams(
            collective_id=0, has_side_effects=True, vmem_limit_bytes=LIMIT_MIB * 1024 * 1024
        ),
    )(amplitudes, oo_vectors, ov_slab.reshape(chunks, CHUNK, width), vv_vectors)
    return pl.pallas_call(
        finish_kernel,
        out_shape=jax.ShapeDtypeStruct((per, nvirt, width), jnp.float32),
        grid=(per, width // FINISH_COLUMNS),
        in_specs=[vmem, vmem, vmem],
        out_specs=pl.BlockSpec((1, nvirt, FINISH_COLUMNS), lambda i, j: (i, 0, j)),
        compiler_params=pltpu.CompilerParams(vmem_limit_bytes=FINISH_MIB * 1024 * 1024),
    )(partial, received, slab).reshape(per * nvirt, width)


def plain(vv_vectors, oo_vectors, ov_slab, amps_all):
    local_count, nvirt = vv_vectors.shape[0], vv_vectors.shape[1]
    window = amps_all[:I_ROWS]
    direct_term = jnp.einsum("ib,pab->pia", window, vv_vectors, preferred_element_type=jnp.float32)
    hole_term = jnp.einsum(
        "pji,ja->pia", oo_vectors[:, :, :I_ROWS], amps_all, preferred_element_type=jnp.float32
    )
    dressed = (direct_term - hole_term).astype(jnp.bfloat16).reshape(local_count, I_ROWS * nvirt)
    regrouped = lax.all_to_all(dressed, ("grp", "vec"), split_axis=1, concat_axis=0, tiled=True)
    return lax.dot_general(
        regrouped,
        lax.all_gather(ov_slab, ("grp", "vec"), axis=0, tiled=True),
        (((0,), (0,)), ((), ())),
        preferred_element_type=jnp.float32,
    )


def solution(mesh):
    ng, nv = mesh.shape["grp"], mesh.shape["vec"]

    def shards(vv_vectors, oo_vectors, ov_slab, amplitudes):
        if I_ROWS % (ng * nv) or vv_vectors.shape[0] % CHUNK or ov_slab.shape[1] % FINISH_COLUMNS:
            amps_all = lax.all_gather(amplitudes, "grp", axis=0, tiled=True)
            return plain(vv_vectors, oo_vectors, ov_slab, amps_all)
        return contract(ng, nv, vv_vectors, oo_vectors, ov_slab, amplitudes)

    return jax.shard_map(
        shards,
        mesh=mesh,
        in_specs=(
            P(("grp", "vec"), None, None),
            P(("grp", "vec"), None, None),
            P(("grp", "vec"), None),
            P("grp", None),
        ),
        out_specs=P(("grp", "vec"), None),
        check_vma=False,
    )
```
